32 devices in a mesh: batch: 8 (over z, core), seq: 4 (over y, x).
Axes of the slice: x: 2, y: 2, z: 4, core: 2. Of those that a mesh axis runs over, the one named last changes fastest.
Arguments:
- tokens: bfloat16 [8, 2048, 768], P('batch', 'seq'), may hold values from -6 to 6
- segments: int32 [8, 2048], P('batch'), may hold values from 0 to 15, never falling along the last dimension, each value on 1 to 1280 neighbouring positions
- qkv_weight: float32 [3, 768, 768], P(None, ('batch', 'seq')), may hold values from -0.21875 to 0.21875
- qv_bias: float32 [2, 768], P(None, ('batch', 'seq')), may hold values from -1.8 to 1.8
- attn_out_weight: float32 [768, 768], P(('batch', 'seq')), may hold values from -1.75 to 1.75
- attn_out_bias: float32 [768], P(('batch', 'seq')), may hold values from -1.8 to 1.8
- norm1_gain: float32 [768], P(('batch', 'seq')), may hold values from 0.5 to 1.5
- norm1_bias: float32 [768], P(('batch', 'seq')), may hold values from -1.8 to 1.8
- up_weight: float32 [768, 3072], P(('batch', 'seq')), may hold values from -0.21875 to 0.21875
- up_bias: float32 [3072], P(('batch', 'seq')), may hold values from -1.8 to 1.8
- down_weight: float32 [3072, 768], P(('batch', 'seq')), may hold values from -0.109375 to 0.109375
- down_bias: float32 [768], P(('batch', 'seq')), may hold values from -1.8 to 1.8
- norm2_gain: float32 [768], P(('batch', 'seq')), may hold values from 0.5 to 1.5
- norm2_bias: float32 [768], P(('batch', 'seq')), may hold values from -1.8 to 1.8
- cotangent: bfloat16 [8, 2048, 768], P('batch', 'seq'), may hold values from -6 to 6
Outputs:
- output: bfloat16 [8, 2048, 768], P('batch', 'seq')
- tokens_grad: bfloat16 [8, 2048, 768], P('batch', 'seq')
- qkv_weight_grad: float32 [3, 768, 768], P(None, ('batch', 'seq'))
- qv_bias_grad: float32 [2, 768], P(None, ('batch', 'seq'))
- attn_out_weight_grad: float32 [768, 768], P(('batch', 'seq'))
- attn_out_bias_grad: float32 [768], P(('batch', 'seq'))
- norm1_gain_grad: float32 [768], P(('batch', 'seq'))
- norm1_bias_grad: float32 [768], P(('batch', 'seq'))
- up_weight_grad: float32 [768, 3072], P(('batch', 'seq'))
- up_bias_grad: float32 [3072], P(('batch', 'seq'))
- down_weight_grad: float32 [3072, 768], P(('batch', 'seq'))
- down_bias_grad: float32 [768], P(('batch', 'seq'))
- norm2_gain_grad: float32 [768], P(('batch', 'seq'))
- norm2_bias_grad: float32 [768], P(('batch', 'seq'))
The draws below stay inside these ranges and needn't reach their ends.
Inputs may be any that keep to these rules, and one draw needn't show every extreme that they name: `segments`: along each sequence the document numbers never fall; every number appears, each as a run of 1 to 1280 tokens, one run exactly 1280.
All inputs are finite; a program needn't handle non-finite values.
Results may differ from the reference program's by a relative error of at most 0.018.
Values may be sent and summed in bfloat16 or wider, within the bound.
A program may use at most 256 MiB of HBM per device.

```python
import math
import jax
import jax.numpy as jnp
import numpy as np
from jax import lax

D = 768
HEADS = 12
HEAD_DIM = 64
FF = 3072
SEQ_LEN = 2048
DOCS = 16
DOC_MOST = 1280
SEQS = 8


def block_levels(rng, extent, pieces, least, top_value):
    def one(position, blocks):
        steps = jax.random.uniform(jax.random.fold_in(jax.random.fold_in(rng, 6), position), (blocks,), jnp.float32, least / len(pieces), top_value / len(pieces))
        return jnp.repeat(jnp.exp(steps), extent[position] // blocks).reshape((-1,) + (1,) * (len(extent) - position - 1))

    gain = one(*pieces[0])
    for cut in pieces[1:]:
        gain = gain * one(*cut)
    return gain


def profile(number_of, total, limit, skew):
    loads = [(1 << 20) // math.isqrt(grade ** skew) + 1 for grade in range(2, number_of + 1)]
    spare, holding = total - limit - (number_of - 1), [1] * (number_of - 1)
    while spare > 0:
        candidates = [i for i in range(number_of - 1) if holding[i] < limit]
        mass, left = sum([loads[i] for i in candidates]), spare
        for i in candidates:
            more = min(limit - holding[i], max(1, left * loads[i] // mass), spare)
            holding[i] = holding[i] + more
            spare = spare - more
    return np.array([limit] + holding)


def ragged_sizes(own_key, number_of, total, bound, slope):
    if number_of == 2:
        one = jax.random.randint(own_key, (), max(1, total - bound), min(bound, total - 1) + 1)
        return jnp.stack([one, total - one])
    lengths = jnp.asarray(profile(number_of, total, bound, slope), jnp.int32)
    twos = (number_of - 1) // 2
    donor, receiver = lengths[1:1 + 2 * twos:2], lengths[2:2 + 2 * twos:2]
    room = jnp.minimum(donor - 1, bound - receiver)
    passed = jax.random.randint(jax.random.fold_in(own_key, 1), (twos,), 0, 1 << 20) % (room + 1)
    lengths = lengths.at[1:1 + 2 * twos:2].set(donor - passed).at[2:2 + 2 * twos:2].set(receiver + passed)
    return lengths[jax.random.permutation(jax.random.fold_in(own_key, 2), number_of)]


def scatter_about(own_key, extent, scale, most, cuts=(), kind=jnp.bfloat16):
    array = jax.random.normal(own_key, extent, jnp.float32) * scale
    if len(cuts) > 0:
        array = block_levels(own_key, extent, cuts, -0.22, 0.18) * array
    return jnp.clip(array, min=-most, max=most).astype(kind)


def setup_inputs(seed: int = 0) -> dict:
    key_of = jax.random.split(jax.random.key(seed), 16)
    return {
        "tokens": scatter_about(key_of[0], (SEQS, SEQ_LEN, D), 1.0, 6.0, ((0, 8), (1, 4))),
        "segments": jax.vmap(lambda own: jnp.searchsorted(jnp.cumsum(ragged_sizes(own, DOCS, SEQ_LEN, DOC_MOST, 2)), jnp.arange(SEQ_LEN), side="right"))(jax.random.split(key_of[1], SEQS)).reshape((SEQS, SEQ_LEN)).astype(jnp.int32),
        "qkv_weight": scatter_about(key_of[2], (3, D, D), D ** -0.5, 0.21875, ((1, 32),), jnp.float32),
        "qv_bias": scatter_about(key_of[3], (2, D), 0.3, 1.8, ((1, 32),), jnp.float32),
        "attn_out_weight": scatter_about(key_of[4], (D, D), (D // 64) ** -0.5, 1.75, ((0, 32),), jnp.float32),
        "attn_out_bias": scatter_about(key_of[5], (D,), 0.3, 1.8, ((0, 32),), jnp.float32),
        "norm1_gain": jnp.clip(1.0 + 0.1 * jax.random.normal(key_of[6], (D,), jnp.float32), 0.5, 1.5),
        "norm1_bias": scatter_about(key_of[7], (D,), 0.3, 1.8, ((0, 32),), jnp.float32),
        "up_weight": scatter_about(key_of[8], (D, FF), D ** -0.5, 0.21875, ((0, 32),), jnp.float32),
        "up_bias": scatter_about(key_of[9], (FF,), 0.3, 1.8, ((0, 32),), jnp.float32),
        "down_weight": scatter_about(key_of[10], (FF, D), FF ** -0.5, 0.109375, ((0, 32),), jnp.float32),
        "down_bias": scatter_about(key_of[11], (D,), 0.3, 1.8, ((0, 32),), jnp.float32),
        "norm2_gain": jnp.clip(1.0 + 0.1 * jax.random.normal(key_of[12], (D,), jnp.float32), 0.5, 1.5),
        "norm2_bias": scatter_about(key_of[13], (D,), 0.3, 1.8, ((0, 32),), jnp.float32),
        "cotangent": scatter_about(key_of[14], (SEQS, SEQ_LEN, D), 1.0, 6.0, ((0, 8), (1, 4))),
    }


@jax.custom_vjp
def low(v):
    return lax.optimization_barrier(v.astype(jnp.bfloat16)).astype(jnp.float32)

@jax.custom_vjp
def low_back(v):
    return v

def low_keep(v):
    return (low(v), None)

def low_pass(kept, grad):
    return (grad,)

def back_keep(v):
    return (v, None)

def back_low(kept, grad):
    return (low(grad),)
low.defvjp(low_keep, low_pass)
low_back.defvjp(back_keep, back_low)
epsilon = 1e-05
masked_score = -1e+30

def matmul(left, right):
    return jnp.dot(left, right, precision=lax.Precision.HIGHEST, preferred_element_type=jnp.float32)

def layer_norm(values, gain_vec, shift_vec):
    centre = lax.optimization_barrier(jnp.mean(values, axis=-1, keepdims=True))
    centred = values - centre
    spread = lax.optimization_barrier(jnp.mean(centred * centred, axis=-1, keepdims=True))
    return centred * lax.rsqrt(spread + epsilon) * gain_vec + shift_vec

def attend_block(queries, query_docs, key_rows, value_rows, key_docs):
    scores = jnp.einsum('qhd,khd->hqk', queries, key_rows, precision=lax.Precision.HIGHEST) / math.sqrt(HEAD_DIM)
    scores = low_back(scores)
    same_doc = (query_docs[:, None] == key_docs[None, :])[None]
    scores = jnp.where(same_doc, scores, masked_score)
    peak = lax.optimization_barrier(jnp.max(scores, axis=-1, keepdims=True))
    weights = jnp.exp(scores - peak)
    probs = weights / lax.optimization_barrier(jnp.sum(weights, axis=-1, keepdims=True))
    probs = low(probs)
    return jnp.einsum('hqk,khd->qhd', probs, value_rows, precision=lax.Precision.HIGHEST)

def one_sequence(rows, documents, params):
    triple, triple_bias, merger, merger_bias, gain_one, shift_one, widener, widen_bias, narrower, narrow_bias, gain_two, shift_two = params
    length = rows.shape[0]
    queries = low_back(low(matmul(rows, triple[0]) + triple_bias[0]))
    key_rows = low_back(low(matmul(rows, triple[1])))
    value_rows = low_back(low(matmul(rows, triple[2]) + triple_bias[1]))
    heads_query = queries.reshape(length, HEADS, HEAD_DIM)
    heads_key = key_rows.reshape(length, HEADS, HEAD_DIM)
    heads_value = value_rows.reshape(length, HEADS, HEAD_DIM)
    block_rows = math.gcd(length, 512)
    blocks = length // block_rows
    checked = jax.checkpoint(attend_block)
    context = lax.map(lambda element: checked(element[0], element[1], heads_key, heads_value, documents), (heads_query.reshape(blocks, block_rows, HEADS, HEAD_DIM), documents.reshape(blocks, block_rows)))
    context = low_back(low(context.reshape(length, HEADS * HEAD_DIM)))
    attn_branch = low_back(matmul(context, merger) + merger_bias)
    hidden = layer_norm(rows + attn_branch, gain_one, shift_one)
    inner = low_back(matmul(low(hidden), widener) + widen_bias)
    act = low(jax.nn.gelu(inner, approximate=False))
    ffn_branch = low_back(matmul(act, narrower) + narrow_bias)
    return layer_norm(hidden + ffn_branch, gain_two, shift_two)

def encoder(inputs, params, segments):
    rounded = jax.tree.map(low, params)
    return lax.map(lambda element: one_sequence(element[0], element[1], rounded), (inputs, segments))

def reference(tokens, segments, qkv_weight, qv_bias, attn_out_weight, attn_out_bias, norm1_gain, norm1_bias, up_weight, up_bias, down_weight, down_bias, norm2_gain, norm2_bias, cotangent):
    params = (qkv_weight, qv_bias, attn_out_weight, attn_out_bias, norm1_gain, norm1_bias, up_weight, up_bias, down_weight, down_bias, norm2_gain, norm2_bias)
    inputs = tokens.astype(jnp.float32)
    output, pullback = jax.vjp(lambda values, weights: encoder(values, weights, segments), inputs, params)
    grad_inputs, grads = pullback(cotangent.astype(jnp.float32))
    return (output.astype(jnp.bfloat16), grad_inputs.astype(jnp.bfloat16), grads[0], grads[1], grads[2], grads[3], grads[4], grads[5], grads[6], grads[7], grads[8], grads[9], grads[10], grads[11])
```

```python
import functools
import math

import jax
import jax.numpy as jnp
from jax import lax
from jax.experimental import pallas as pl
from jax.experimental.pallas import tpu as pltpu
from jax.sharding import PartitionSpec as P

HEAD_DIM = 64
epsilon = 1e-05
masked_score = -1e30
F32 = jnp.float32
BF16 = jnp.bfloat16
ANY = pl.BlockSpec(memory_space=pl.ANY)
INV = pl.BlockSpec(memory_space=pltpu.VMEM)
INS = pl.BlockSpec(memory_space=pltpu.SMEM)


def dot_nn(a, b):
    return lax.dot_general(a, b, (((1,), (0,)), ((), ())), preferred_element_type=F32)


def dot_nt(a, b):
    return lax.dot_general(a, b, (((1,), (1,)), ((), ())), preferred_element_type=F32)


def dot_tn(a, b):
    return lax.dot_general(a, b, (((0,), (0,)), ((), ())), preferred_element_type=F32)


def turn_docs(doc_row_ref, doc_turned, span, block):
    doc_turned[span, :] = jnp.broadcast_to(doc_row_ref[:, span], (128, block)).T


def doc_column(doc_turned, span, block):
    docs = doc_turned[span, :]
    return jnp.concatenate([docs] * (block // 128), axis=1)


def attend_kernel(
    heads, block, low_ref, high_ref, rows_ref, weight_ref, bias_ref, doc_row_ref,
    query_ref, key_ref, value_ref, context_ref, turned_ref, log_ref,
    value_turned, doc_turned, scores,
):
    length, width = rows_ref.shape
    wide = heads * HEAD_DIM
    count = length // block

    def project(i, carry):
        span = pl.ds(pl.multiple_of(i * block, block), block)
        rows = rows_ref[span, :]
        turn_docs(doc_row_ref, doc_turned, span, block)
        for part in range(3):
            made = dot_nn(rows, weight_ref[part]) + bias_ref[part][None, :]
            made = made.astype(BF16)
            if part == 0:
                made = made * jnp.asarray(HEAD_DIM ** (-0.5), BF16)
            if part == 2:
                value_turned[:, span] = made.T
            target = (query_ref, key_ref, value_ref)[part]
            for h in range(heads):
                target[h, span, :] = made[:, h * HEAD_DIM : (h + 1) * HEAD_DIM]
        return carry

    lax.fori_loop(0, count, project, 0)

    def one_block(i, carry):
        span = pl.ds(pl.multiple_of(i * block, block), block)
        query_docs = doc_row_ref[:, span]
        queries = [query_ref[h, span, :] for h in range(heads)]

        def score(j, peaks):
            keys_at = pl.ds(pl.multiple_of(j * block, block), block)
            same = doc_column(doc_turned, keys_at, block) == query_docs
            out = []
            for h in range(heads):
                value = jnp.where(same, dot_nt(key_ref[h, keys_at, :], queries[h]), masked_score)
                scores[h, keys_at, :] = value
                out.append(jnp.maximum(peaks[h], jnp.max(value.reshape(-1, 8, block), axis=0)))
            return tuple(out)

        first = (jnp.full((8, block), masked_score, F32),) * heads
        peaks = lax.fori_loop(low_ref[i], high_ref[i], score, first)
        peaks = [jnp.max(peak, axis=0, keepdims=True) for peak in peaks]

        def absorb(j, state):
            keys_at = pl.ds(pl.multiple_of(j * block, block), block)
            out = []
            for h in range(heads):
                total, context = state[2 * h : 2 * h + 2]
                weights = jnp.exp(scores[h, keys_at, :] - peaks[h])
                total = total + jnp.sum(weights.reshape(-1, 8, block), axis=0)
                context = context + dot_nn(
                    value_turned[h * HEAD_DIM : (h + 1) * HEAD_DIM, keys_at], weights.astype(BF16)
                )
                out += [total, context]
            return tuple(out)

        start = (jnp.zeros((8, block), F32), jnp.zeros((HEAD_DIM, block), F32)) * heads
        state = lax.fori_loop(low_ref[i], high_ref[i], absorb, start)
        for h in range(heads):
            total = jnp.sum(state[2 * h], axis=0, keepdims=True)
            turned_ref[h * HEAD_DIM : (h + 1) * HEAD_DIM, span] = state[2 * h + 1] / total
            log_ref[h : h + 1, span] = peaks[h] + jnp.log(total)
        context_ref[span, :] = turned_ref[:, span].T.astype(BF16)
        return carry

    lax.fori_loop(0, count, one_block, 0)


def attend(rows, weight, bias, docs, low, high, block):
    length, width = rows.shape
    wide = weight.shape[2]
    heads = wide // HEAD_DIM
    shape = jax.ShapeDtypeStruct
    return pl.pallas_call(
        functools.partial(attend_kernel, heads, block),
        out_shape=(
            shape((heads, length, HEAD_DIM), BF16),
            shape((heads, length, HEAD_DIM), BF16),
            shape((heads, length, HEAD_DIM), BF16),
            shape((length, wide), BF16),
            shape((wide, length), F32),
            shape((heads, length), F32),
        ),
        in_specs=[INS, INS, INV, INV, INV, INV],
        out_specs=(INV,) * 6,
        scratch_shapes=[
            pltpu.VMEM((wide, length), BF16),
            pltpu.VMEM((length, 128), jnp.int32),
            pltpu.VMEM((heads, length, block), F32),
        ],
        compiler_params=pltpu.CompilerParams(vmem_limit_bytes=60 << 20),
        name="attend",
    )(low, high, rows, weight, bias, docs.reshape(1, length))


def attend_back_kernel(
    heads, block, low_ref, high_ref, rows_ref, weight_ref, doc_row_ref,
    query_ref, key_ref, value_ref, turned_ref, log_ref, grad_ref,
    part_ref, weight_grad_ref, bias_grad_ref,
    query_turned, key_turned, grad_heads, delta, joined, doc_turned,
):
    length, width = rows_ref.shape
    wide = heads * HEAD_DIM
    count = length // block

    def prepare(i, carry):
        span = pl.ds(pl.multiple_of(i * block, block), block)
        turn_docs(doc_row_ref, doc_turned, span, block)
        grad = grad_ref[span, :]
        turned = grad.astype(F32).T
        product = turned * turned_ref[:, span]
        for h in range(heads):
            part = slice(h * HEAD_DIM, (h + 1) * HEAD_DIM)
            delta[h : h + 1, span] = jnp.sum(product[part, :], axis=0, keepdims=True)
            grad_heads[h, span, :] = grad[:, part]
            key_turned[part, span] = key_ref[h, span, :].T
        query_turned[:, span] = jnp.zeros((wide, block), F32)
        return carry

    lax.fori_loop(0, count, prepare, 0)

    def one_block(j, carry):
        keys_at = pl.ds(pl.multiple_of(j * block, block), block)
        key_docs = doc_column(doc_turned, keys_at, block)
        keys = [key_ref[h, keys_at, :] for h in range(heads)]
        values = [value_ref[h, keys_at, :] for h in range(heads)]

        def absorb(i, state):
            span = pl.ds(pl.multiple_of(i * block, block), block)
            same = key_docs == doc_row_ref[:, span]
            out = []
            for h in range(heads):
                part = slice(h * HEAD_DIM, (h + 1) * HEAD_DIM)
                grad_key, grad_value = state[2 * h : 2 * h + 2]
                queries = query_ref[h, span, :]
                grads = grad_heads[h, span, :]
                scores = dot_nt(keys[h], queries)
                probs = jnp.where(same, jnp.exp(scores - log_ref[h : h + 1, span]), 0.0)
                grad_probs = dot_nt(values[h], grads)
                grad_scores = (probs * (grad_probs - delta[h : h + 1, span])).astype(BF16)
                grad_value = grad_value + dot_nn(probs.astype(BF16), grads)
                grad_key = grad_key + dot_nn(grad_scores, queries)
                query_turned[part, span] += dot_nn(key_turned[part, keys_at], grad_scores)
                out += [grad_key, grad_value]
            return tuple(out)

        start = (jnp.zeros((block, HEAD_DIM), F32),) * (2 * heads)
        state = lax.fori_loop(low_ref[j], high_ref[j], absorb, start)
        grad_key = jnp.concatenate(state[0::2], axis=1)
        grad_value = jnp.concatenate(state[1::2], axis=1)
        joined[1, keys_at, :] = grad_key.astype(BF16)
        joined[2, keys_at, :] = grad_value.astype(BF16)
        return carry

    lax.fori_loop(0, count, one_block, 0)

    def finish(i, sums):
        span = pl.ds(pl.multiple_of(i * block, block), block)
        grad_query = (query_turned[:, span].T * (HEAD_DIM ** (-0.5))).astype(BF16)
        joined[0, span, :] = grad_query
        rows = dot_nt(grad_query, weight_ref[0])
        rows = rows + dot_nt(joined[1, span, :], weight_ref[1])
        rows = rows + dot_nt(joined[2, span, :], weight_ref[2])
        part_ref[span, :] = rows.astype(BF16)
        return (
            sums[0] + jnp.sum(grad_query.astype(F32), axis=0, keepdims=True),
            sums[1] + jnp.sum(joined[2, span, :].astype(F32), axis=0, keepdims=True),
        )

    zero = jnp.zeros((1, wide), F32)
    sums = lax.fori_loop(0, count, finish, (zero, zero))
    bias_grad_ref[0:1, :] = sums[0]
    bias_grad_ref[1:2, :] = sums[1]
    tile = 256

    def weight_rows(i, carry):
        at = pl.ds(pl.multiple_of(i * tile, tile), tile)
        turned = rows_ref[:, at].T
        for part in range(3):
            weight_grad_ref[part, at, :] = dot_nn(turned, joined[part]).astype(BF16)
        return carry

    lax.fori_loop(0, width // tile, weight_rows, 0)


def attend_back(rows, weight, docs, low, high, query, key, value, turned, log, grad, block):
    length, width = rows.shape
    wide = weight.shape[2]
    heads = wide // HEAD_DIM
    shape = jax.ShapeDtypeStruct
    return pl.pallas_call(
        functools.partial(attend_back_kernel, heads, block),
        out_shape=(
            shape((length, width), BF16),
            shape((3, width, wide), BF16),
            shape((2, wide), F32),
        ),
        in_specs=[INS, INS] + [INV] * 9,
        out_specs=(INV,) * 3,
        scratch_shapes=[
            pltpu.VMEM((wide, length), F32),
            pltpu.VMEM((wide, length), BF16),
            pltpu.VMEM((heads, length, HEAD_DIM), BF16),
            pltpu.VMEM((heads, length), F32),
            pltpu.VMEM((3, length, wide), BF16),
            pltpu.VMEM((length, 128), jnp.int32),
        ],
        compiler_params=pltpu.CompilerParams(vmem_limit_bytes=60 << 20),
        name="attend_back",
    )(
        low, high, rows, weight, docs.reshape(1, length),
        query, key, value, turned, log, grad,
    )


def normalize(values):
    centre = jnp.mean(values, axis=-1, keepdims=True)
    centred = values - centre
    spread = jnp.mean(centred * centred, axis=-1, keepdims=True)
    scale = lax.rsqrt(spread + epsilon)
    return centred * scale, scale


def normalize_back(grad, normal, scale):
    first = jnp.mean(grad, axis=-1, keepdims=True)
    second = jnp.mean(grad * normal, axis=-1, keepdims=True)
    return scale * (grad - first - normal * second)


def add_rows(values):
    return jnp.sum(values, axis=0, keepdims=True)


def dense_kernel(
    step, chunk, context_ref, tokens_ref, cotangent_ref, vector_ref, wide_ref,
    merger_hbm, widener_hbm, narrower_hbm,
    output_ref, grad_context_ref, grad_mid_ref, grad_merger_ref, grad_widener_ref,
    grad_narrower_ref, sums_ref, wide_sum_ref,
    merger, widener, narrower, hidden, hidden_low, normal_one, scale_one, act, slope, branch,
    mid_two, grad_ffn, sems,
):
    rows, width = tokens_ref.shape
    inner = widener.shape[1]
    pieces = inner // chunk
    steps = rows // step
    copies = [
        pltpu.make_async_copy(merger_hbm, merger, sems.at[0]),
        pltpu.make_async_copy(widener_hbm, widener, sems.at[1]),
        pltpu.make_async_copy(narrower_hbm, narrower, sems.at[2]),
    ]
    for copy in copies:
        copy.start()
    merger_bias, gain_one, shift_one, narrow_bias, gain_two, shift_two = (
        vector_ref[i : i + 1, :] for i in range(6)
    )
    sums_ref[...] = jnp.zeros_like(sums_ref)
    wide_sum_ref[...] = jnp.zeros_like(wide_sum_ref)
    copies[0].wait()
    for i in range(steps):
        span = slice(i * step, (i + 1) * step)
        mid = tokens_ref[span, :].astype(F32) + (
            dot_nn(context_ref[span, :], merger[...]) + merger_bias
        )
        normal, scale = normalize(mid)
        normal_one[span, :] = normal
        scale_one[span, :] = scale
        value = normal * gain_one + shift_one
        hidden[span, :] = value
        hidden_low[span, :] = value.astype(BF16)
    copies[1].wait()
    copies[2].wait()
    branch[...] = jnp.zeros_like(branch)

    def widen(j, carry):
        at = pl.ds(pl.multiple_of(j * chunk, chunk), chunk)
        bias = wide_ref[:, at]
        for i in range(steps):
            span = slice(i * step, (i + 1) * step)
            value = dot_nn(hidden_low[span, :], widener[:, at]) + bias
            half = 0.5 + 0.5 * lax.erf(value * (2.0 ** -0.5))
            low = (value * half).astype(BF16)
            act[span, at] = low
            slope[span, at] = (
                half + value * (jnp.exp(-0.5 * value * value) * (1.0 / math.sqrt(2.0 * math.pi)))
            ).astype(slope.dtype)
            branch[span, :] += dot_nn(low, narrower[at, :])
        return carry

    lax.fori_loop(0, pieces, widen, 0)
    for i in range(steps):
        span = slice(i * step, (i + 1) * step)
        normal, scale = normalize(hidden[span, :] + (branch[span, :] + narrow_bias))
        output_ref[span, :] = (normal * gain_two + shift_two).astype(BF16)
        grad = cotangent_ref[span, :].astype(F32)
        grad_mid = normalize_back(grad * gain_two, normal, scale)
        mid_two[span, :] = grad_mid
        low = grad_mid.astype(BF16)
        grad_ffn[span, :] = low
        sums_ref[3:4, :] += add_rows(low.astype(F32))
        sums_ref[4:5, :] += add_rows(grad * normal)
        sums_ref[5:6, :] += add_rows(grad)

    def narrow_back(j, carry):
        at = pl.ds(pl.multiple_of(j * chunk, chunk), chunk)
        grad_narrower_ref[at, :] = dot_tn(act[:, at], grad_ffn[...]).astype(grad_narrower_ref.dtype)
        total = jnp.zeros((1, chunk), F32)
        for i in range(steps):
            span = slice(i * step, (i + 1) * step)
            value = dot_nt(grad_ffn[span, :], narrower[at, :]) * slope[span, at].astype(F32)
            low = value.astype(BF16)
            total = total + add_rows(low.astype(F32))
            act[span, at] = low
            mid_two[span, :] += dot_nt(low, widener[:, at])
        wide_sum_ref[:, at] = total
        grad_widener_ref[:, at] = dot_tn(hidden_low[...], act[:, at]).astype(grad_widener_ref.dtype)
        return carry

    lax.fori_loop(0, pieces, narrow_back, 0)
    for i in range(steps):
        span = slice(i * step, (i + 1) * step)
        grad = mid_two[span, :]
        normal = normal_one[span, :]
        grad_mid = normalize_back(grad * gain_one, normal, scale_one[span, :])
        grad_mid_ref[span, :] = grad_mid
        low = grad_mid.astype(BF16)
        grad_ffn[span, :] = low
        sums_ref[0:1, :] += add_rows(low.astype(F32))
        sums_ref[1:2, :] += add_rows(grad * normal)
        sums_ref[2:3, :] += add_rows(grad)
        grad_context_ref[span, :] = dot_nt(low, merger[...]).astype(BF16)
    grad_merger_ref[...] = dot_tn(context_ref[...], grad_ffn[...]).astype(grad_merger_ref.dtype)


def dense(context, tokens, cotangent, vectors, wide_bias, merger, widener, narrower):
    rows, width = tokens.shape
    inner = widener.shape[1]
    shape = jax.ShapeDtypeStruct
    return pl.pallas_call(
        functools.partial(dense_kernel, 256, 512),
        out_shape=(
            shape((rows, width), BF16),
            shape((rows, width), BF16),
            shape((rows, width), F32),
            shape((width, width), BF16),
            shape((width, inner), BF16),
            shape((inner, width), BF16),
            shape((8, width), F32),
            shape((1, inner), F32),
        ),
        in_specs=[INV] * 5 + [ANY] * 3,
        out_specs=(INV,) * 8,
        scratch_shapes=[
            pltpu.VMEM((width, width), BF16),
            pltpu.VMEM((width, inner), BF16),
            pltpu.VMEM((inner, width), BF16),
            pltpu.VMEM((rows, width), F32),
            pltpu.VMEM((rows, width), BF16),
            pltpu.VMEM((rows, width), F32),
            pltpu.VMEM((rows, 1), F32),
            pltpu.VMEM((rows, inner), BF16),
            pltpu.VMEM((rows, inner), BF16),
            pltpu.VMEM((rows, width), F32),
            pltpu.VMEM((rows, width), F32),
            pltpu.VMEM((rows, width), BF16),
            pltpu.SemaphoreType.DMA((3,)),
        ],
        compiler_params=pltpu.CompilerParams(vmem_limit_bytes=63 << 20),
        name="dense",
    )(context, tokens, cotangent, vectors, wide_bias, merger, widener, narrower)


def block_ranges(docs, block):
    grouped = docs.reshape(-1, block)
    low = jnp.sum((docs[None, :] < grouped[:, :1]).astype(jnp.int32), axis=1) // block
    high = jnp.sum((docs[None, :] <= grouped[:, -1:]).astype(jnp.int32), axis=1)
    return low, (high + block - 1) // block


def spread(parts):
    return jnp.transpose(parts, (1, 0, 2)).reshape(parts.shape[1], -1)


class PlainLinks:
    def __init__(self, mesh, seqs):
        self.groups = mesh.shape["seq"] // seqs
        self.seqs = seqs

    def place(self):
        me = lax.axis_index("seq")
        return me // self.groups, me % self.groups

    def fetch(self, tokens, triple, small, merger, widener, narrower):
        both = ("batch", "seq")
        seq, group = self.place()
        wide = triple.shape[2] // self.groups
        rows = lax.all_gather(tokens, "seq", axis=1, tiled=True)
        rows = lax.dynamic_index_in_dim(rows, seq, 0, keepdims=False)
        triple = lax.all_gather(triple, both, axis=1, tiled=True)
        triple = lax.dynamic_slice_in_dim(triple, group * wide, wide, 2)
        return (
            rows,
            triple,
            lax.all_gather(small, both, axis=0, tiled=False),
            lax.all_gather(merger, both, axis=0, tiled=True),
            lax.all_gather(widener, both, axis=0, tiled=True),
            lax.all_gather(narrower, both, axis=0, tiled=True),
        )

    def to_rows(self, part):
        count = self.seqs * self.groups
        length, wide = part.shape
        parts = lax.all_to_all(part.reshape(count, length // count, wide), "seq", 0, 0)
        parts = parts.reshape(self.seqs, self.groups, length // count, wide)
        return jnp.transpose(parts, (0, 2, 1, 3)).reshape(-1, self.groups * wide)

    def to_groups(self, rows):
        count = self.seqs * self.groups
        parts = rows.reshape(self.seqs, -1, self.groups, rows.shape[1] // self.groups)
        parts = jnp.transpose(parts, (0, 2, 1, 3)).reshape(count, parts.shape[1], parts.shape[3])
        parts = lax.all_to_all(parts, "seq", 0, 0)
        return parts.reshape(-1, parts.shape[2])

    def settle(self, part, triple, small, merger, widener, narrower):
        both = ("batch", "seq")
        seq, group = self.place()
        length, width = part.shape
        rows = jnp.zeros((self.seqs, length, width), part.dtype)
        rows = lax.dynamic_update_index_in_dim(rows, part, seq, 0)
        rows = lax.psum_scatter(rows, "seq", scatter_dimension=1, tiled=True)
        full = jnp.zeros(triple.shape[:2] + (triple.shape[2] * self.groups,), triple.dtype)
        full = lax.dynamic_update_slice_in_dim(full, triple, group * triple.shape[2], 2)
        return (
            rows.reshape(-1, width),
            lax.psum_scatter(full, both, scatter_dimension=1, tiled=True),
            lax.psum_scatter(small, both, scatter_dimension=0, tiled=False),
            lax.psum_scatter(merger, both, scatter_dimension=0, tiled=True),
            lax.psum_scatter(widener, both, scatter_dimension=0, tiled=True),
            lax.psum_scatter(narrower, both, scatter_dimension=0, tiled=True),
        )


def on_device(
    links, tokens, segments, qkv_weight, qv_bias, attn_out_weight, attn_out_bias, norm1_gain,
    norm1_bias, up_weight, up_bias, down_weight, down_bias, norm2_gain, norm2_bias, cotangent,
):
    seqs, rows, width = tokens.shape
    piece = attn_out_bias.shape[0]
    ratio = up_bias.shape[0] // piece
    block = 256
    seq, group = links.place()
    wide = width // links.groups
    small = jnp.concatenate(
        [qv_bias, jnp.stack([attn_out_bias, norm1_gain, norm1_bias, down_bias, norm2_gain, norm2_bias]),
         up_bias.reshape(ratio, piece)], axis=0,
    )
    full, triple, small, merger, widener, narrower = links.fetch(
        tokens, qkv_weight.astype(BF16), small.astype(BF16),
        attn_out_weight.astype(BF16), up_weight.astype(BF16), down_weight.astype(BF16),
    )
    vectors = spread(small[:, :8]).astype(F32)
    wide_bias = small[:, 8:].reshape(1, -1).astype(F32)
    biases = lax.dynamic_slice_in_dim(vectors[:2], group * wide, wide, 1)
    biases = jnp.stack([biases[0], jnp.zeros_like(biases[0]), biases[1]])
    docs = lax.dynamic_index_in_dim(segments, seq, 0, keepdims=False)
    low, high = block_ranges(docs, block)
    query, key, value, context, turned, log = attend(full, triple, biases, docs, low, high, block)
    output, grad_context, grad_mid, grad_merger, grad_widener, grad_narrower, sums, wide_sum = dense(
        links.to_rows(context), tokens.reshape(-1, width), cotangent.reshape(-1, width),
        vectors[2:], wide_bias, merger, widener, narrower,
    )
    part, grad_triple, bias_sums = attend_back(
        full, triple, docs, low, high, query, key, value, turned, log,
        links.to_groups(grad_context), block,
    )
    bias_full = jnp.zeros((2, width), F32)
    bias_full = lax.dynamic_update_slice_in_dim(bias_full, bias_sums, group * wide, 1)
    owners = width // piece
    small_sums = jnp.concatenate([bias_full, sums[:6]], axis=0).reshape(8, owners, piece)
    small_sums = jnp.concatenate(
        [jnp.transpose(small_sums, (1, 0, 2)), wide_sum.reshape(owners, ratio, piece)], axis=1
    )
    grad_rows, grad_triple, small_sums, grad_merger, grad_widener, grad_narrower = links.settle(
        part, grad_triple, small_sums, grad_merger, grad_widener, grad_narrower
    )
    grad_rows = (grad_rows.astype(F32) + grad_mid).astype(BF16)
    return (
        output.reshape(tokens.shape),
        grad_rows.reshape(tokens.shape),
        grad_triple.astype(F32),
        small_sums[:2],
        grad_merger.astype(F32),
        small_sums[2],
        small_sums[3],
        small_sums[4],
        grad_widener.astype(F32),
        small_sums[8:].reshape(-1),
        grad_narrower.astype(F32),
        small_sums[5],
        small_sums[6],
        small_sums[7],
    )


def solution(mesh):
    both = ("batch", "seq")
    token = P("batch", "seq", None)
    matrix = P(both, None)
    vector = P(both)
    weights = (
        P(None, both, None), P(None, both), matrix, vector, vector, vector,
        matrix, vector, matrix, vector, vector, vector,
    )

    def program(tokens, *rest):
        links = PlainLinks(mesh, tokens.shape[0])
        return on_device(links, tokens, *rest)

    return jax.shard_map(
        program,
        mesh=mesh,
        in_specs=(token, P("batch", None)) + weights + (token,),
        out_specs=(token, token) + weights,
        check_vma=False,
    )
```
